128 devices in a mesh: row: 8 (over y_lo, x), col: 16 (over y_hi, z, core).
Axes of the slice: x: 4, y: 4 (y_hi: 2, y_lo: 2; y = y_hi * 2 + y_lo), z: 4, core: 2. Of those that a mesh axis runs over, the one named last changes fastest.
Arguments:
- factor_panel: bfloat16 [12288, 98304], P('row', 'col'), may hold values from -1 to 1, as said below
- normals: bfloat16 [98304, 128], P(('col', 'row')), may hold values from -6 to 6
- bond_vectors: float32 [3, 4096, 12], P(None, ('col', 'row')), may hold values from -9 to 9
- neighbours: int32 [4096, 12], P(('col', 'row')), may hold values from 0 to 175
- send_atoms: int32 [128, 16], P(('col', 'row')), may hold values from 0 to 31
- radial_weight: bfloat16 [128, 128], replicated, may hold values from -1.5 to 1.5
- radial_bias: float32 [128], replicated, may hold values from -3 to 3
- middle_weight: bfloat16 [128, 128], replicated, may hold values from -0.5 to 0.5
- middle_bias: float32 [128], replicated, may hold values from -3 to 3
- output_weight: float32 [128], replicated, may hold values from -0.5 to 0.5
Outputs:
- atom_energy: float32 [4096, 128], P(('col', 'row'))
- forces: float32 [3, 4096, 128], P(None, ('col', 'row'))
The draws below stay inside these ranges and needn't reach their ends.
Inputs may be any that keep to these rules, and one draw needn't show every extreme that they name: `factor_panel`: entries above the factor's diagonal are zero.
All inputs are finite; a program needn't handle non-finite values.
Results may differ from the reference program's by a relative error of at most 0.0052.
Values may be sent and summed in bfloat16 or wider, within the bound.
A program may use at most 128 MiB of HBM per device.

```python
import math
import jax
import jax.numpy as jnp
from jax import lax

ORDER = 98304
SAMPLES = 128
TILE = 16
DOMAIN_ATOMS = 32
NEIGHBOURS = 12
RADIAL = 128
UNITS = 128
SENT_ATOMS = 16
POOL = 176
PANEL_LOCAL = 1536
PANEL_ROWS = 12288
LOCAL_COLS = 6144
DOMAINS = 128
ATOMS = 4096
N_ROW = 8
N_COL = 16


def draw_factor_panel(key, part):
    row_ids = jnp.arange(PANEL_ROWS, dtype=jnp.int32)
    process_row = row_ids // PANEL_LOCAL
    local_row = row_ids % PANEL_LOCAL
    panel_row = (local_row // TILE * N_ROW + process_row) * TILE + local_row % TILE
    global_row = ORDER - PANEL_ROWS + panel_row
    col_ids = jnp.arange(ORDER, dtype=jnp.int32)
    process_col = col_ids // LOCAL_COLS
    local_col = col_ids % LOCAL_COLS
    global_col = (local_col // TILE * N_COL + process_col) * TILE + local_col % TILE
    values = jax.random.normal(key, (PANEL_ROWS, ORDER), jnp.float32)
    scaled = values * (0.2 / math.sqrt(ORDER))
    lower = global_col[None, :] <= global_row[:, None]
    diagonal = global_col[None, :] == global_row[:, None]
    result = jnp.where(lower, scaled, 0.0) + jnp.where(diagonal, 0.15, 0.0)
    return result.astype(jnp.bfloat16)


def touch_ends(drawn, rng, low, high):
    spot = [jax.random.randint(jax.random.fold_in(rng, axis), (), 0, length) for axis, length in enumerate(drawn.shape)]
    longest = drawn.shape.index(max(drawn.shape))
    beside = spot[:longest] + [(spot[longest] + 1) % drawn.shape[longest]] + spot[longest + 1:]
    return drawn.at[tuple(spot)].set(low).at[tuple(beside)].set(high)


def levels(stream_key, dims, shards, smallest, top_value):
    loudness, own = 1.0, jax.random.fold_in(stream_key, 6)
    for position, parts in shards:
        draws = jnp.exp(jax.random.uniform(jax.random.fold_in(own, position), (parts,), jnp.float32, smallest / len(shards), top_value / len(shards)))
        loudness = loudness * jnp.repeat(draws, dims[position] // parts).reshape([-1 if axis == position else 1 for axis in range(len(dims))])
    return loudness


def noise(own_key, shape, scale, bound, cuts=(), kind=jnp.bfloat16):
    values = jax.random.normal(own_key, shape, jnp.float32) * scale
    if len(cuts) > 0:
        values = levels(own_key, shape, cuts, -0.22, 0.18) * values
    return jnp.clip(values, min=-bound, max=bound).astype(kind)


def setup_inputs(seed: int = 0) -> dict:
    key_list = jax.random.split(jax.random.key(seed), 11)
    factor_panel = draw_factor_panel(jax.random.fold_in(key_list[10], 71), 0)
    normals = noise(key_list[1], (ORDER, SAMPLES), 1.0, 6.0, ((0, 128),))
    bond_vectors = noise(key_list[2], (3, ATOMS, NEIGHBOURS), 1.5, 9.0, ((1, 128),), jnp.float32)
    neighbours = touch_ends(jax.random.randint(key_list[3], (ATOMS, NEIGHBOURS), 0, POOL), jax.random.fold_in(key_list[3], 1), 0, POOL - 1).astype(jnp.int32)
    send_atoms = touch_ends(jax.random.randint(key_list[4], (DOMAINS, SENT_ATOMS), 0, DOMAIN_ATOMS), jax.random.fold_in(key_list[4], 1), 0, DOMAIN_ATOMS - 1).astype(jnp.int32)
    radial_weight = noise(key_list[5], (RADIAL, UNITS), (RADIAL // 8) ** -0.5, 1.5)
    radial_bias = noise(key_list[6], (UNITS,), 0.5, 3.0, (), jnp.float32)
    middle_weight = noise(key_list[7], (UNITS, UNITS), UNITS ** -0.5, 0.5)
    middle_bias = noise(key_list[8], (UNITS,), 0.5, 3.0, (), jnp.float32)
    output_weight = noise(key_list[9], (UNITS,), UNITS ** -0.5, 0.5, (), jnp.float32)
    return dict(factor_panel=factor_panel, normals=normals, bond_vectors=bond_vectors, neighbours=neighbours, send_atoms=send_atoms, radial_weight=radial_weight, radial_bias=radial_bias, middle_weight=middle_weight, middle_bias=middle_bias, output_weight=output_weight)


def rounded(values):
    return lax.optimization_barrier(values.astype(jnp.bfloat16)).astype(jnp.float32)


def pair_terms(own_disp, near_disp, bond_block, radial_weight, radial_bias, middle_weight, middle_bias, output_weight):
    vectors = bond_block[:, :, :, None] + near_disp - own_disp[:, :, None, :]
    squared = jnp.sum(vectors * vectors, axis=0)
    count = radial_weight.shape[0]
    centres = 30.0 * jnp.arange(count, dtype=jnp.float32) / (count - 1)
    spread = 90.0 / (count - 1)
    scaled = (squared[..., None] - centres) / spread
    basis = jnp.exp(-scaled * scaled)
    flat_basis = basis.reshape(-1, count)
    flat_scaled = scaled.reshape(-1, count)
    radial_full = radial_weight.astype(jnp.float32)
    middle_full = middle_weight.astype(jnp.float32)
    highest = lax.Precision.HIGHEST
    first = jnp.tanh(jnp.dot(rounded(flat_basis), radial_full, precision=highest) + radial_bias)
    second = jnp.tanh(jnp.dot(rounded(first), middle_full, precision=highest) + middle_bias)
    energies = jnp.sum(second * output_weight, axis=-1)
    back_second = rounded((1.0 - second * second) * output_weight)
    back_first = rounded(jnp.dot(back_second, middle_full.T, precision=highest) * (1.0 - first * first))
    radial_grad = jnp.dot(back_first, radial_full.T, precision=highest)
    slopes = jnp.sum(radial_grad * flat_basis * (-2.0 / spread) * flat_scaled, axis=-1)
    shape = squared.shape
    atom_part = 0.5 * jnp.sum(energies.reshape(shape), axis=1)
    force_part = 2.0 * jnp.sum(slopes.reshape(shape)[None] * vectors, axis=2)
    return atom_part, force_part


def reference(factor_panel, normals, bond_vectors, neighbours, send_atoms, radial_weight, radial_bias, middle_weight, middle_bias, output_weight):
    block = math.gcd(PANEL_ROWS, 512)
    right_side = normals.astype(jnp.float32)
    pieces = factor_panel.reshape(PANEL_ROWS // block, block, ORDER)
    stored = lax.map(lambda piece: jnp.dot(piece.astype(jnp.float32), right_side, precision=lax.Precision.HIGHEST), pieces)
    stored = stored.reshape(PANEL_ROWS, SAMPLES)
    panel = stored.reshape(N_ROW, PANEL_LOCAL // TILE, TILE, SAMPLES).transpose(1, 0, 2, 3).reshape(PANEL_ROWS, SAMPLES)
    displacements = panel.reshape(DOMAINS, 3, DOMAIN_ATOMS, SAMPLES).transpose(1, 0, 2, 3).reshape(3, ATOMS, SAMPLES)
    domain_ids = jnp.arange(DOMAINS, dtype=jnp.int32)
    grid_row = domain_ids % N_ROW
    grid_col = domain_ids // N_ROW
    members = [domain_ids[:, None] * DOMAIN_ATOMS + jnp.arange(DOMAIN_ATOMS, dtype=jnp.int32)[None, :]]
    for row_step in (-1, 0, 1):
        for col_step in (-1, 0, 1):
            other = ((grid_col + col_step) % N_COL) * N_ROW + (grid_row + row_step) % N_ROW
            members.append(other[:, None] * DOMAIN_ATOMS + send_atoms[other])
    pool_table = jnp.concatenate(members, axis=1)
    owner_rows = pool_table[jnp.arange(ATOMS, dtype=jnp.int32) // DOMAIN_ATOMS]
    partner = jnp.take_along_axis(owner_rows, neighbours, axis=1)
    nearby = displacements[:, partner, :]
    block_count = ATOMS // 8
    own_blocks = displacements.reshape(3, block_count, 8, SAMPLES).transpose(1, 0, 2, 3)
    near_blocks = nearby.reshape(3, block_count, 8, NEIGHBOURS, SAMPLES).transpose(1, 0, 2, 3, 4)
    bond_blocks = bond_vectors.reshape(3, block_count, 8, NEIGHBOURS).transpose(1, 0, 2, 3)
    energy_blocks, force_blocks = lax.map(
        lambda items: pair_terms(items[0], items[1], items[2], radial_weight, radial_bias, middle_weight, middle_bias, output_weight),
        (own_blocks, near_blocks, bond_blocks))
    atom_energy = energy_blocks.reshape(ATOMS, SAMPLES)
    forces = force_blocks.transpose(1, 0, 2, 3).reshape(3, ATOMS, SAMPLES)
    return atom_energy, forces
```

```python
import functools
import math

import jax
import jax.numpy as jnp
from jax import lax
from jax.experimental import pallas as pl
from jax.experimental.pallas import tpu as pltpu
from jax.sharding import PartitionSpec as P

MESH = pl.DeviceIdType.MESH


def remote(src, dst, send, recv, device):
    return pltpu.make_async_remote_copy(src_ref=src, dst_ref=dst, send_sem=send, recv_sem=recv, device_id=device, device_id_type=MESH)


def displacement_kernel(sent_ref, factor_ref, normals_ref, pool_ref, fbuf, nbuf, acc, pbuf, sbuf, rbuf, disp, hsend, pool,
                        fsem, nsem, gsend, grecv, psend, precv, rsend, rrecv, tsend, trecv, hsends, hrecv, y_ready, z_ready, core_ready):
    p, q = lax.axis_index("row"), lax.axis_index("col")
    x, y_lo = lax.rem(p, 4), p // 4
    core, z, y_hi = lax.rem(q, 2), lax.rem(q // 2, 4), q // 8
    at_x = lambda step: y_lo * 4 + lax.rem(x + step, 4)
    other = lambda place: lax.rem(place + 4, 8)
    xp, xm, x2 = at_x(1), at_x(3), at_x(2)
    order = [p, xm, xp, other(p), x2, other(xm), other(xp), other(x2)]
    depth = normals_ref.shape[0]
    half = depth // 2

    own = pltpu.make_async_copy(normals_ref, nbuf.at[p], nsem)
    own.start()
    loads = []
    for k, place in enumerate(order):
        columns = pl.ds(pl.multiple_of(place * depth, depth), depth)
        loads.append(pltpu.make_async_copy(factor_ref.at[:, columns], fbuf.at[k], fsem.at[k]))
        loads[-1].start()

    x_ring = [(at_x(s), q) for s in (1, 2, 3)]
    z_ring = [(p, y_hi * 8 + lax.rem(z + s, 4) * 2 + core) for s in (1, 2, 3)]
    q_flip = lax.rem(q + 8, 16)
    y_ring = [(other(p), q), (p, q_flip), (other(p), q_flip)]
    partner = (p, q + 1 - 2 * core)
    barrier = pltpu.get_barrier_semaphore()
    for device in (*x_ring, *y_ring, *z_ring, partner):
        pl.semaphore_signal(barrier, inc=1, device_id=device, device_id_type=MESH)
    pl.semaphore_wait(barrier, 10)
    for device in y_ring:
        pl.semaphore_signal(y_ready, inc=1, device_id=device, device_id_type=MESH)

    sends = []

    def part(place, h):
        return nbuf.at[place, pl.ds(h * half, half)]

    def push(place, h, device):
        n = len(sends)
        copy = remote(part(place, h), part(place, h), gsend.at[n], grecv.at[place, h], device)
        copy.start()
        sends.append(copy)

    def arrive(place, h):
        remote(part(place, h), part(place, h), gsend.at[0], grecv.at[place, h], (p, q)).wait_recv()

    to_xp, to_xm, to_y = (xp, q), (xm, q), (other(p), q)
    own.wait()
    push(p, 0, to_xp)
    push(p, 1, to_xm)
    push(p, 0, to_y)
    push(p, 1, to_xp)
    push(p, 0, to_xm)
    push(p, 1, to_y)

    def multiply(k):
        place = order[k]
        loads[k].wait()

        def block(m, carry):
            rows = pl.ds(pl.multiple_of(m * 192, 192), 192)
            out = jnp.dot(fbuf[k, rows, :], nbuf[place], preferred_element_type=jnp.float32).reshape(2, 96, 128)
            acc[m] = out if k == 0 else acc[m] + out
            return carry

        lax.fori_loop(0, 8, block, 0)

    multiply(0)
    arrive(xm, 0)
    push(xm, 0, to_xp)
    arrive(xp, 1)
    push(xp, 1, to_xm)
    for h in (0, 1):
        arrive(other(p), h)
        push(other(p), h, to_xp)
        push(other(p), h, to_xm)
    arrive(xm, 1)
    multiply(1)
    arrive(xp, 0)
    multiply(2)
    pl.semaphore_wait(y_ready, 3)
    for device in z_ring:
        pl.semaphore_signal(z_ready, inc=1, device_id=device, device_id_type=MESH)
    arrive(x2, 0)
    push(x2, 0, to_y)
    arrive(x2, 1)
    push(x2, 1, to_y)
    multiply(3)
    multiply(4)
    pl.semaphore_wait(z_ready, 3)
    pl.semaphore_signal(core_ready, inc=1, device_id=partner, device_id_type=MESH)
    for h in (0, 1):
        arrive(other(xm), h)
    multiply(5)
    for h in (0, 1):
        arrive(other(xp), h)
    multiply(6)
    for h in (0, 1):
        arrive(other(x2), h)
    multiply(7)

    pair = remote(acc.at[:, 1 - core], pbuf, psend, precv, partner)
    pair.start()
    pl.semaphore_wait(core_ready, 1)
    pair.wait_recv()

    group = q // 2

    def spread(step, carry):
        m = lax.rem(group + step, 8)
        sbuf[m] = (acc[m, core] + pbuf[m]).reshape(6, 16, 128)
        for j in range(6):
            tile = 8 * j + p
            owner, place = tile // 6, lax.rem(tile, 6)
            remote(sbuf.at[m, j], rbuf.at[group, place], rsend.at[m], rrecv.at[group], (owner, 2 * m + core)).start()
        return carry

    lax.fori_loop(1, 8, spread, 0)
    sbuf[group] = (acc[group, core] + pbuf[group]).reshape(6, 16, 128)
    for j in range(6):
        tile = 8 * j + p
        owner, place = tile // 6, lax.rem(tile, 6)

        @pl.when(owner == p)
        def _():
            pltpu.make_async_copy(sbuf.at[group, j], rbuf.at[group, place], trecv.at[place]).start()

        @pl.when(owner != p)
        def _():
            remote(sbuf.at[group, j], rbuf.at[group, place], tsend.at[j], trecv.at[place], (owner, q)).start()

    for i in range(6):
        pltpu.make_async_copy(sbuf.at[group, 0], rbuf.at[group, i], trecv.at[i]).wait()

    def landed(step, carry):
        m = lax.rem(group + step, 8)
        remote(sbuf.at[m], rbuf.at[m], rsend.at[m], rrecv.at[m], (p, q)).wait_recv()
        return carry

    lax.fori_loop(1, 8, landed, 0)
    total = rbuf[0]
    for m in range(1, 8):
        total = total + rbuf[m]
    total = total.reshape(96, 128)
    disp[...] = total
    for c in range(3):
        pool[c, 0:32] = total[c * 32:(c + 1) * 32]
        for h in range(16):
            hsend[c, pl.ds(h, 1)] = disp[pl.ds(c * 32 + sent_ref[h], 1), :]
    halos = []
    for u in (-1, 0, 1):
        for v in (-1, 0, 1):
            slot = (u + 1) * 3 + v + 1
            if u == 0 and v == 0:
                pool[:, 32 + 16 * slot:48 + 16 * slot] = hsend[...]
                continue
            device = (lax.rem(p - u + 8, 8), lax.rem(q - v + 16, 16))
            halos.append(remote(hsend, pool.at[:, pl.ds(32 + 16 * slot, 16)], hsends.at[slot], hrecv.at[slot], device))
            halos[-1].start()
    for copy in halos:
        copy.wait_recv()
    pool_ref[...] = pool[...]
    for copy in halos:
        copy.wait_send()
    for copy in sends:
        copy.wait_send()
    pair.wait_send()

    def drained(step, carry):
        m = lax.rem(group + step, 8)
        remote(sbuf.at[m], rbuf.at[m], rsend.at[m], rrecv.at[m], (p, q)).wait_send()
        return carry

    lax.fori_loop(1, 8, drained, 0)
    for j in range(6):

        @pl.when((8 * j + p) // 6 != p)
        def _():
            remote(sbuf.at[group, j], rbuf.at[group, 0], tsend.at[j], trecv.at[0], (p, q)).wait_send()


def displacement_pool(factor_panel, normals, send_atoms):
    f32, bf16 = jnp.float32, jnp.bfloat16
    dma, regular = pltpu.SemaphoreType.DMA, pltpu.SemaphoreType.REGULAR
    rows, cols = factor_panel.shape
    depth, samples = normals.shape
    return pl.pallas_call(
        displacement_kernel,
        out_shape=jax.ShapeDtypeStruct((3, 176, samples), f32),
        in_specs=[pl.BlockSpec(memory_space=pltpu.SMEM), pl.BlockSpec(memory_space=pl.ANY), pl.BlockSpec(memory_space=pl.ANY)],
        out_specs=pl.BlockSpec(memory_space=pltpu.VMEM),
        scratch_shapes=[
            pltpu.VMEM((8, rows, depth), bf16), pltpu.VMEM((8, depth, samples), bf16),
            pltpu.VMEM((8, 2, 96, samples), f32), pltpu.VMEM((8, 96, samples), f32),
            pltpu.VMEM((8, 6, 16, samples), f32), pltpu.VMEM((8, 6, 16, samples), f32),
            pltpu.VMEM((96, samples), f32), pltpu.VMEM((3, 16, samples), f32), pltpu.VMEM((3, 176, samples), f32),
            dma((8,)), dma, dma((14,)), dma((8, 2)), dma, dma, dma((8,)), dma((8,)), dma((6,)), dma((6,)), dma((9,)), dma((9,)),
            regular, regular, regular,
        ],
        compiler_params=pltpu.CompilerParams(collective_id=0, has_side_effects=True, vmem_limit_bytes=48 * 2**20),
        name="displacements",
    )(send_atoms.reshape(-1), factor_panel, normals)


OMEGA = 90.0 / 127.0
SCALE = math.sqrt(math.log2(math.e)) / OMEGA
MU = 30.0 / 127.0


def pair_kernel(width, nb_ref, bond_ref, pool_ref, w1t_ref, w2t_ref, w2_ref, w1_ref, cols_ref,
                energy_ref, force_ref, vec_ref):
    atoms = energy_ref.shape[0]
    count = nb_ref.shape[0] // atoms
    per = width // 128

    def atom(i, carry):
        own = [pool_ref[c, pl.ds(i, 1), :] for c in range(3)]
        energy = jnp.zeros((1, 128), jnp.float32)
        force = [jnp.zeros((1, 128), jnp.float32) for _ in range(3)]
        muc = cols_ref[0]
        b1 = cols_ref[1]
        b2 = cols_ref[2]
        ow = cols_ref[3]
        if per > 1:
            muc, b1, b2, ow = [jnp.concatenate([v] * per, axis=1) for v in (muc, b1, b2, ow)]
        for g in range(count // per):
            rows = []
            vecs = []
            for h in range(per):
                n = i * count + g * per + h
                idx = nb_ref[n]
                vec = [pool_ref[c, pl.ds(idx, 1), :] + (bond_ref[c, n] - own[c]) for c in range(3)]
                vecs.append(vec)
                rows.append((vec[0] * vec[0] + vec[1] * vec[1] + vec[2] * vec[2]) * SCALE)
            sq = jnp.concatenate(rows, axis=1) if per > 1 else rows[0]
            t = sq - muc
            basis = jnp.exp2(-(t * t))
            first = jnp.tanh(jnp.dot(w1t_ref[...], basis.astype(jnp.bfloat16), preferred_element_type=jnp.float32) + b1)
            second = jnp.tanh(jnp.dot(w2t_ref[...], first.astype(jnp.bfloat16), preferred_element_type=jnp.float32) + b2)
            so = second * ow
            phi = jnp.sum(so, axis=0, keepdims=True)
            back2 = (ow - second * so).astype(jnp.bfloat16)
            back1 = (jnp.dot(w2_ref[...], back2, preferred_element_type=jnp.float32) * (1.0 - first * first)).astype(jnp.bfloat16)
            grad = jnp.dot(w1_ref[...], back1, preferred_element_type=jnp.float32)
            slope = jnp.sum(grad * (basis * t), axis=0, keepdims=True)
            for h in range(per):
                energy = energy + phi[:, h * 128:(h + 1) * 128]
                for c in range(3):
                    force[c] = force[c] + slope[:, h * 128:(h + 1) * 128] * vecs[h][c]
        energy_ref[pl.ds(i, 1), :] = 0.5 * energy
        for c in range(3):
            force_ref[c, pl.ds(i, 1), :] = force[c] * (2.0 * -2.0 / (OMEGA * OMEGA * SCALE))
        return carry

    lax.fori_loop(0, atoms, atom, 0)


def pair_stage(pool, bond, nb, w1, b1, w2, b2, ow, width=1536):
    atoms = bond.shape[1]
    samples = pool.shape[2]
    cols = jnp.stack([jnp.arange(128, dtype=jnp.float32) * (MU * SCALE), b1, b2, ow])
    cols = jnp.broadcast_to(cols[:, :, None], (4, 128, 128))
    V = pl.BlockSpec(memory_space=pltpu.VMEM)
    S = pl.BlockSpec(memory_space=pltpu.SMEM)
    return pl.pallas_call(
        functools.partial(pair_kernel, width),
        out_shape=(jax.ShapeDtypeStruct((atoms, samples), jnp.float32), jax.ShapeDtypeStruct((3, atoms, samples), jnp.float32)),
        in_specs=[S, S, V, V, V, V, V, V],
        out_specs=(V, V),
        scratch_shapes=[pltpu.VMEM((3, 384, 128), jnp.float32)],
        name="pairs",
    )(nb.reshape(-1), bond.reshape(3, -1), pool, w1.T, w2.T, w2, w1, cols)


def per_device(factor_panel, normals, bond_vectors, neighbours, send_atoms, radial_weight, radial_bias, middle_weight, middle_bias, output_weight):
    pool = displacement_pool(factor_panel, normals, send_atoms)
    return pair_stage(pool, bond_vectors, neighbours, radial_weight, radial_bias, middle_weight, middle_bias, output_weight)


def solution(mesh):
    whole = P(("col", "row"), None)
    return jax.shard_map(
        per_device,
        mesh=mesh,
        in_specs=(P("row", "col"), whole, P(None, ("col", "row"), None), whole, whole, P(), P(), P(), P(), P()),
        out_specs=(whole, P(None, ("col", "row"), None)),
        check_vma=False,
    )
```

```python
import functools
import math

import jax
import jax.numpy as jnp
from jax import lax
from jax.experimental import pallas as pl
from jax.experimental.pallas import tpu as pltpu
from jax.sharding import PartitionSpec as P

MESH = pl.DeviceIdType.MESH


def remote(src, dst, send, recv, device):
    return pltpu.make_async_remote_copy(src_ref=src, dst_ref=dst, send_sem=send, recv_sem=recv, device_id=device, device_id_type=MESH)


def displacement_kernel(sent_hbm, factor_ref, normals_ref, pool_ref, fbuf, nbuf, acc, pbuf, sbuf, rbuf, disp, hsend, pool,
                        fsem, nsem, gsend, grecv, psend, precv, rsend, rrecv, tsend, trecv, hsends, hrecv, y_ready, z_ready, core_ready, sent_ref, sent_sem):
    p, q = lax.axis_index("row"), lax.axis_index("col")
    x, y_lo = lax.rem(p, 4), p // 4
    core, z, y_hi = lax.rem(q, 2), lax.rem(q // 2, 4), q // 8
    at_x = lambda step: y_lo * 4 + lax.rem(x + step, 4)
    other = lambda place: lax.rem(place + 4, 8)
    xp, xm, x2 = at_x(1), at_x(3), at_x(2)
    order = [p, xm, xp, other(p), x2, other(xm), other(xp), other(x2)]
    depth = normals_ref.shape[0]
    half = depth // 2

    own = pltpu.make_async_copy(normals_ref, nbuf.at[p], nsem)
    own.start()
    sent_in = pltpu.make_async_copy(sent_hbm, sent_ref, sent_sem)
    sent_in.start()
    loads = []
    for k, place in enumerate(order):
        columns = pl.ds(pl.multiple_of(place * depth, depth), depth)
        loads.append([pltpu.make_async_copy(factor_ref.at[:, side, :, columns], fbuf.at[k, part], fsem.at[k, part])
                      for part, side in enumerate((1 - core, core))])
        for copy in loads[-1]:
            copy.start()

    x_ring = [(at_x(s), q) for s in (1, 2, 3)]
    z_ring = [(p, y_hi * 8 + lax.rem(z + s, 4) * 2 + core) for s in (1, 2, 3)]
    q_flip = lax.rem(q + 8, 16)
    y_ring = [(other(p), q), (p, q_flip), (other(p), q_flip)]
    partner = (p, q + 1 - 2 * core)
    barrier = pltpu.get_barrier_semaphore()
    for device in (*x_ring, *y_ring, *z_ring, partner):
        pl.semaphore_signal(barrier, inc=1, device_id=device, device_id_type=MESH)
    pl.semaphore_wait(barrier, 10)
    for device in y_ring:
        pl.semaphore_signal(y_ready, inc=1, device_id=device, device_id_type=MESH)

    sends = []

    def part(place, h):
        return nbuf.at[place, pl.ds(h * half, half)]

    def push(place, h, device):
        n = len(sends)
        copy = remote(part(place, h), part(place, h), gsend.at[n], grecv.at[place, h], device)
        copy.start()
        sends.append(copy)

    def arrive(place, h):
        remote(part(place, h), part(place, h), gsend.at[0], grecv.at[place, h], (p, q)).wait_recv()

    to_xp, to_xm, to_y = (xp, q), (xm, q), (other(p), q)
    own.wait()
    push(p, 0, to_xp)
    push(p, 1, to_xm)
    push(p, 0, to_y)
    push(p, 1, to_xp)
    push(p, 0, to_xm)
    push(p, 1, to_y)

    def product(k, part):
        weights = nbuf[order[k]]
        out = jnp.dot(fbuf[k, part].reshape(768, depth), weights, preferred_element_type=jnp.float32).reshape(8, 96, 128)
        acc[part] = out if k == 0 else acc[part] + out

    def multiply(k):
        for copy in loads[k]:
            copy.wait()

        def half_rows(part, carry):
            product(k, part)
            return carry

        lax.fori_loop(0, 2, half_rows, 0)

    multiply(0)
    arrive(xm, 0)
    push(xm, 0, to_xp)
    arrive(xp, 1)
    push(xp, 1, to_xm)
    for h in (0, 1):
        arrive(other(p), h)
        push(other(p), h, to_xp)
        push(other(p), h, to_xm)
    arrive(xm, 1)
    multiply(1)
    arrive(xp, 0)
    multiply(2)
    pl.semaphore_wait(y_ready, 3)
    for device in z_ring:
        pl.semaphore_signal(z_ready, inc=1, device_id=device, device_id_type=MESH)
    arrive(x2, 0)
    push(x2, 0, to_y)
    arrive(x2, 1)
    push(x2, 1, to_y)
    multiply(3)
    multiply(4)
    pl.semaphore_wait(z_ready, 3)
    pl.semaphore_signal(core_ready, inc=1, device_id=partner, device_id_type=MESH)
    for h in (0, 1):
        arrive(other(xm), h)
    multiply(5)
    for h in (0, 1):
        arrive(other(xp), h)
    multiply(6)
    for h in (0, 1):
        arrive(other(x2), h)
    for copy in loads[7]:
        copy.wait()
    group = q // 2

    def ahead(step):
        late = step // 4
        shift = (1 - late) * lax.rem(2 + step, 4) + late * (1 + lax.rem(step, 3))
        return lax.rem(y_hi + 1 - late, 2) * 4 + lax.rem(z + shift, 4)

    def swap(m):
        return remote(acc.at[0, m], pbuf.at[m], psend.at[m], precv.at[m], partner)

    product(7, 0)

    def swap_out(step, carry):
        swap(ahead(step)).start()
        return carry

    lax.fori_loop(0, 7, swap_out, 0)
    swap(group).start()
    product(7, 1)
    pl.semaphore_wait(core_ready, 1)

    def spread(step, carry):
        m = ahead(step)
        swap(m).wait_recv()
        sbuf[m] = (acc[1, m] + pbuf[m]).reshape(6, 16, 128)
        for j in range(6):
            tile = 8 * j + p
            owner, place = tile // 6, lax.rem(tile, 6)
            remote(sbuf.at[m, j], rbuf.at[group, place], rsend.at[m], rrecv.at[group], (owner, 2 * m + core)).start()
        return carry

    lax.fori_loop(0, 7, spread, 0)
    swap(group).wait_recv()
    sbuf[group] = (acc[1, group] + pbuf[group]).reshape(6, 16, 128)
    for j in range(6):
        tile = 8 * j + p
        owner, place = tile // 6, lax.rem(tile, 6)

        @pl.when(owner == p)
        def _():
            pltpu.make_async_copy(sbuf.at[group, j], rbuf.at[group, place], trecv.at[place]).start()

        @pl.when(owner != p)
        def _():
            remote(sbuf.at[group, j], rbuf.at[group, place], tsend.at[j], trecv.at[place], (owner, q)).start()

    for i in range(6):
        pltpu.make_async_copy(sbuf.at[group, 0], rbuf.at[group, i], trecv.at[i]).wait()

    def landed(step, carry):
        m = lax.rem(group + step, 8)
        remote(sbuf.at[m], rbuf.at[m], rsend.at[m], rrecv.at[m], (p, q)).wait_recv()
        return carry

    lax.fori_loop(1, 8, landed, 0)
    sent_in.wait()
    total = rbuf[0]
    for m in range(1, 8):
        total = total + rbuf[m]
    total = total.reshape(96, 128)
    disp[...] = total
    for c in range(3):
        pool[c, 0:32] = total[c * 32:(c + 1) * 32]
        for h in range(16):
            hsend[c, pl.ds(h, 1)] = disp[pl.ds(c * 32 + sent_ref[0, h], 1), :]
    halos = []
    for u in (-1, 0, 1):
        for v in (-1, 0, 1):
            slot = (u + 1) * 3 + v + 1
            if u == 0 and v == 0:
                pool[:, 32 + 16 * slot:48 + 16 * slot] = hsend[...]
                continue
            device = (lax.rem(p - u + 8, 8), lax.rem(q - v + 16, 16))
            halos.append(remote(hsend, pool.at[:, pl.ds(32 + 16 * slot, 16)], hsends.at[slot], hrecv.at[slot], device))
            halos[-1].start()
    for copy in halos:
        copy.wait_recv()
    pool_ref[...] = pool[...]
    for copy in halos:
        copy.wait_send()
    for copy in sends:
        copy.wait_send()
    for m in range(8):
        swap(m).wait_send()

    def drained(step, carry):
        m = lax.rem(group + step, 8)
        remote(sbuf.at[m], rbuf.at[m], rsend.at[m], rrecv.at[m], (p, q)).wait_send()
        return carry

    lax.fori_loop(1, 8, drained, 0)
    for j in range(6):

        @pl.when((8 * j + p) // 6 != p)
        def _():
            remote(sbuf.at[group, j], rbuf.at[group, 0], tsend.at[j], trecv.at[0], (p, q)).wait_send()


def displacement_pool(factor_panel, normals, send_atoms):
    f32, bf16 = jnp.float32, jnp.bfloat16
    dma, regular = pltpu.SemaphoreType.DMA, pltpu.SemaphoreType.REGULAR
    rows, cols = factor_panel.shape
    depth, samples = normals.shape
    return pl.pallas_call(
        displacement_kernel,
        out_shape=jax.ShapeDtypeStruct((3, 176, samples), f32),
        in_specs=[pl.BlockSpec(memory_space=pltpu.HBM), pl.BlockSpec(memory_space=pltpu.HBM), pl.BlockSpec(memory_space=pltpu.HBM)],
        out_specs=pl.BlockSpec(memory_space=pltpu.VMEM),
        scratch_shapes=[
            pltpu.VMEM((8, 2, 8, 96, depth), bf16), pltpu.VMEM((8, depth, samples), bf16),
            pltpu.VMEM((2, 8, 96, samples), f32), pltpu.VMEM((8, 96, samples), f32),
            pltpu.VMEM((8, 6, 16, samples), f32), pltpu.VMEM((8, 6, 16, samples), f32),
            pltpu.VMEM((96, samples), f32), pltpu.VMEM((3, 16, samples), f32), pltpu.VMEM((3, 176, samples), f32),
            dma((8, 2)), dma, dma((14,)), dma((8, 2)), dma((8,)), dma((8,)), dma((8,)), dma((8,)), dma((6,)), dma((6,)), dma((9,)), dma((9,)),
            regular, regular, regular, pltpu.SMEM((1, 16), jnp.int32), dma,
        ],
        compiler_params=pltpu.CompilerParams(collective_id=0, has_side_effects=True, vmem_limit_bytes=48 * 2**20),
        name="displacements",
    )(pltpu.with_memory_space_constraint(send_atoms, pltpu.HBM), factor_panel.reshape(8, 2, 96, cols), pltpu.with_memory_space_constraint(normals, pltpu.HBM))


OMEGA = 90.0 / 127.0
SCALE = math.sqrt(math.log2(math.e)) / OMEGA
MU = 30.0 / 127.0


def pieces(column):
    high = column.astype(jnp.bfloat16)
    rest = column - high.astype(jnp.float32)
    middle = rest.astype(jnp.bfloat16)
    low = (rest - middle.astype(jnp.float32)).astype(jnp.bfloat16)
    return high, middle, low


def beside(weights_t, bias):
    place = lax.broadcasted_iota(jnp.int32, (128, 128), 1)
    high, middle, low = [v.astype(jnp.float32) for v in pieces(bias)]
    extra = jnp.where(place == 0, high, jnp.where(place == 1, middle, jnp.where(place == 2, low, 0.0)))
    return jnp.concatenate([weights_t, extra.astype(jnp.bfloat16)], axis=1)[:, :144]


def pair_kernel(group, split, offset, nb_ref, bond_ref, pool_ref, w1_ref, b1_ref, w2_ref, b2_ref, ow_ref,
                energy_ref, force_ref, muc_ref, ow_s, w1a, w2a):
    atoms = energy_ref.shape[0]
    count = nb_ref.shape[0]
    bf16, f32 = jnp.bfloat16, jnp.float32
    spread = lambda ref: jnp.broadcast_to(ref[...].reshape(1, 128), (128, 128))
    muc_ref[...] = lax.broadcasted_iota(jnp.int32, (128, 128), 0).astype(f32) * (MU * SCALE)
    ow_s[...] = spread(ow_ref).T
    w1a[...] = beside(w1_ref[...].T, spread(b1_ref).T)
    w2a[...] = beside(w2_ref[...].T, spread(b2_ref).T)
    wide = count * 128
    tile = lambda v: jnp.concatenate([v] * (wide // 128), axis=1)
    dot = functools.partial(jnp.dot, preferred_element_type=f32)
    ones = jnp.where(lax.broadcasted_iota(jnp.int32, (16, wide), 0) < 3, 1.0, 0.0).astype(bf16)
    dense = lambda w, v: dot(w[...], jnp.concatenate([v.astype(bf16), ones], axis=0))

    def work(i, pairs):
        own = [pool_ref[c, pl.ds(i, 1), :] for c in range(3)]
        rows, vecs = [], []
        for n in pairs:
            idx = nb_ref[n, i]
            vec = [pool_ref[c, pl.ds(idx, 1), :] + (bond_ref[c, n, i] - own[c]) for c in range(3)]
            vecs.append(vec)
            rows.append((vec[0] * vec[0] + vec[1] * vec[1] + vec[2] * vec[2]) * SCALE)
        tile = lambda v: jnp.concatenate([v] * len(pairs), axis=1)
        ones = jnp.where(lax.broadcasted_iota(jnp.int32, (16, 128 * len(pairs)), 0) < 3, 1.0, 0.0).astype(bf16)
        dense = lambda w, v: dot(w[...], jnp.concatenate([v.astype(bf16), ones], axis=0))
        t = jnp.concatenate(rows, axis=1) - tile(muc_ref[...])
        yield
        basis = jnp.exp2(-(t * t))
        yield
        bt = basis * t
        z1 = dense(w1a, basis)
        yield
        first = jnp.tanh(z1)
        yield
        z2 = dense(w2a, first)
        yield
        second = jnp.tanh(z2)
        yield
        ow = tile(ow_s[...])
        so = second * ow
        back2 = (ow - second * so).astype(bf16)
        phi = jnp.sum(so, axis=0, keepdims=True)
        yield
        back1 = (dot(w2_ref[...], back2) * (1.0 - first * first)).astype(bf16)
        yield
        slope = jnp.sum(dot(w1_ref[...], back1) * bt, axis=0, keepdims=True)
        at = lambda v, n: v[:, n * 128:(n + 1) * 128]
        energy = sum(at(phi, n) for n in range(len(pairs)))
        force = [sum(at(slope, n) * vecs[n][c] for n in range(len(pairs))) for c in range(3)]
        sums[i_key(i)].append((energy, force))
        yield

    sums = {}
    keys = []

    def i_key(i):
        return [k for k, v in keys if v is i][0]

    def run(items, offset):
        gens = [work(i, p) for i, p in items]
        for step in range(9 + offset * (len(gens) - 1)):
            for g, gen in enumerate(gens):
                if 0 <= step - offset * g < 9:
                    next(gen)

    def body(k, carry):
        sums.clear()
        keys.clear()
        items = []
        for a in range(group):
            i = k * group + a
            keys.append((a, i))
            sums[a] = []
            per = count // split
            for h in range(split):
                items.append((i, range(h * per, (h + 1) * per)))
        run(items, offset)
        for a, i in keys:
            energy = sum(v[0] for v in sums[a])
            energy_ref[pl.ds(i, 1), :] = 0.5 * energy
            for c in range(3):
                force_ref[c, pl.ds(i, 1), :] = sum(v[1][c] for v in sums[a]) * (-4.0 / (OMEGA * OMEGA * SCALE))
        return carry

    lax.fori_loop(0, atoms // group, body, 0)


def pair_stage(pool, bond, nb, w1, b1, w2, b2, ow, group=2, split=1, offset=0):
    atoms = bond.shape[1]
    samples = pool.shape[2]
    V = pl.BlockSpec(memory_space=pltpu.VMEM)
    S = pl.BlockSpec(memory_space=pltpu.SMEM)
    f32, bf16 = jnp.float32, jnp.bfloat16
    return pl.pallas_call(
        functools.partial(pair_kernel, group, split, offset),
        out_shape=(jax.ShapeDtypeStruct((atoms, samples), f32), jax.ShapeDtypeStruct((3, atoms, samples), f32)),
        in_specs=[S, S, V, V, V, V, V, V],
        out_specs=(V, V),
        scratch_shapes=[pltpu.VMEM((128, 128), f32)] * 2 + [pltpu.VMEM((128, 144), bf16)] * 2,
        compiler_params=pltpu.CompilerParams(vmem_limit_bytes=16 * 2**20),
        name="pairs",
    )(nb.T, bond.transpose(0, 2, 1), pool, w1, b1, w2, b2, ow)


def per_device(factor_panel, normals, bond_vectors, neighbours, send_atoms, radial_weight, radial_bias, middle_weight, middle_bias, output_weight):
    pool = displacement_pool(factor_panel, normals, send_atoms)
    return pair_stage(pool, bond_vectors, neighbours, radial_weight, radial_bias, middle_weight, middle_bias, output_weight)


def solution(mesh):
    whole = P(("col", "row"), None)
    return jax.shard_map(
        per_device,
        mesh=mesh,
        in_specs=(P("row", "col"), whole, P(None, ("col", "row"), None), whole, whole, P(), P(), P(), P(), P()),
        out_specs=(whole, P(None, ("col", "row"), None)),
        check_vma=False,
    )
```

```python
import functools
import math

import jax
import jax.numpy as jnp
from jax import lax
from jax.experimental import pallas as pl
from jax.experimental.pallas import tpu as pltpu
from jax.sharding import PartitionSpec as P

MESH = pl.DeviceIdType.MESH


def remote(src, dst, send, recv, device):
    return pltpu.make_async_remote_copy(src_ref=src, dst_ref=dst, send_sem=send, recv_sem=recv, device_id=device, device_id_type=MESH)


def displacement_kernel(sent_hbm, factor_ref, normals_ref, pool_ref, fbuf, nbuf, acc, pbuf, sbuf, rbuf, disp, hsend, pool,
                        fsem, nsem, gsend, grecv, psend, precv, rsend, rrecv, tsend, trecv, hsends, hrecv, y_ready, z_ready, core_ready, sent_ref, sent_sem):
    p, q = lax.axis_index("row"), lax.axis_index("col")
    x, y_lo = lax.rem(p, 4), p // 4
    core, z, y_hi = lax.rem(q, 2), lax.rem(q // 2, 4), q // 8
    at_x = lambda step: y_lo * 4 + lax.rem(x + step, 4)
    other = lambda place: lax.rem(place + 4, 8)
    xp, xm, x2 = at_x(1), at_x(3), at_x(2)
    order = [p, xm, xp, other(p), x2, other(xm), other(xp), other(x2)]
    depth = normals_ref.shape[0]
    half = depth // 2

    own = pltpu.make_async_copy(normals_ref, nbuf.at[p], nsem)
    own.start()
    sent_in = pltpu.make_async_copy(sent_hbm, sent_ref, sent_sem)
    sent_in.start()
    loads = []
    for k, place in enumerate(order):
        columns = pl.ds(pl.multiple_of(place * depth, depth), depth)
        loads.append([pltpu.make_async_copy(factor_ref.at[:, side, :, columns], fbuf.at[k, part], fsem.at[k, part])
                      for part, side in enumerate((1 - core, core))])
        for copy in loads[-1]:
            copy.start()

    x_ring = [(at_x(s), q) for s in (1, 2, 3)]
    z_ring = [(p, y_hi * 8 + lax.rem(z + s, 4) * 2 + core) for s in (1, 2, 3)]
    q_flip = lax.rem(q + 8, 16)
    y_ring = [(other(p), q), (p, q_flip), (other(p), q_flip)]
    partner = (p, q + 1 - 2 * core)
    barrier = pltpu.get_barrier_semaphore()
    for device in (*x_ring, *y_ring, *z_ring, partner):
        pl.semaphore_signal(barrier, inc=1, device_id=device, device_id_type=MESH)
    pl.semaphore_wait(barrier, 10)
    for device in y_ring:
        pl.semaphore_signal(y_ready, inc=1, device_id=device, device_id_type=MESH)

    sends = []

    def part(place, h):
        return nbuf.at[place, pl.ds(h * half, half)]

    def push(place, h, device):
        n = len(sends)
        copy = remote(part(place, h), part(place, h), gsend.at[n], grecv.at[place, h], device)
        copy.start()
        sends.append(copy)

    def arrive(place, h):
        remote(part(place, h), part(place, h), gsend.at[0], grecv.at[place, h], (p, q)).wait_recv()

    to_xp, to_xm, to_y = (xp, q), (xm, q), (other(p), q)
    own.wait()
    push(p, 0, to_xp)
    push(p, 1, to_xm)
    push(p, 0, to_y)
    push(p, 1, to_xp)
    push(p, 0, to_xm)
    push(p, 1, to_y)

    def product(k, part):
        weights = nbuf[order[k]]
        out = jnp.dot(fbuf[k, part].reshape(768, depth), weights, preferred_element_type=jnp.float32).reshape(8, 96, 128)
        acc[part] = out if k == 0 else acc[part] + out

    def multiply(k):
        for copy in loads[k]:
            copy.wait()

        def half_rows(part, carry):
            product(k, part)
            return carry

        lax.fori_loop(0, 2, half_rows, 0)

    multiply(0)
    arrive(xm, 0)
    push(xm, 0, to_xp)
    arrive(xp, 1)
    push(xp, 1, to_xm)
    for h in (0, 1):
        arrive(other(p), h)
        push(other(p), h, to_xp)
        push(other(p), h, to_xm)
    arrive(xm, 1)
    multiply(1)
    arrive(xp, 0)
    multiply(2)
    pl.semaphore_wait(y_ready, 3)
    for device in z_ring:
        pl.semaphore_signal(z_ready, inc=1, device_id=device, device_id_type=MESH)
    arrive(x2, 0)
    push(x2, 0, to_y)
    arrive(x2, 1)
    push(x2, 1, to_y)
    multiply(3)
    multiply(4)
    pl.semaphore_wait(z_ready, 3)
    pl.semaphore_signal(core_ready, inc=1, device_id=partner, device_id_type=MESH)
    for h in (0, 1):
        arrive(other(xm), h)
    multiply(5)
    for h in (0, 1):
        arrive(other(xp), h)
    multiply(6)
    for h in (0, 1):
        arrive(other(x2), h)
    for copy in loads[7]:
        copy.wait()
    group = q // 2

    def ahead(step):
        late = step // 4
        shift = (1 - late) * lax.rem(2 + step, 4) + late * (1 + lax.rem(step, 3))
        return lax.rem(y_hi + 1 - late, 2) * 4 + lax.rem(z + shift, 4)

    def swap(m):
        return remote(acc.at[0, m], pbuf.at[m], psend.at[m], precv.at[m], partner)

    product(7, 0)

    def swap_out(step, carry):
        swap(ahead(step)).start()
        return carry

    lax.fori_loop(0, 7, swap_out, 0)
    swap(group).start()
    product(7, 1)
    pl.semaphore_wait(core_ready, 1)

    def spread(step, carry):
        m = ahead(step)
        swap(m).wait_recv()
        sbuf[m] = (acc[1, m] + pbuf[m]).reshape(6, 16, 128)
        for j in range(6):
            tile = 8 * j + p
            owner, place = tile // 6, lax.rem(tile, 6)
            remote(sbuf.at[m, j], rbuf.at[group, place], rsend.at[m], rrecv.at[group], (owner, 2 * m + core)).start()
        return carry

    lax.fori_loop(0, 7, spread, 0)
    swap(group).wait_recv()
    sbuf[group] = (acc[1, group] + pbuf[group]).reshape(6, 16, 128)
    for j in range(6):
        tile = 8 * j + p
        owner, place = tile // 6, lax.rem(tile, 6)

        @pl.when(owner == p)
        def _():
            pltpu.make_async_copy(sbuf.at[group, j], rbuf.at[group, place], trecv.at[place]).start()

        @pl.when(owner != p)
        def _():
            remote(sbuf.at[group, j], rbuf.at[group, place], tsend.at[j], trecv.at[place], (owner, q)).start()

    for i in range(6):
        pltpu.make_async_copy(sbuf.at[group, 0], rbuf.at[group, i], trecv.at[i]).wait()

    def landed(step, carry):
        m = lax.rem(group + step, 8)
        remote(sbuf.at[m], rbuf.at[m], rsend.at[m], rrecv.at[m], (p, q)).wait_recv()
        return carry

    lax.fori_loop(1, 8, landed, 0)
    sent_in.wait()
    total = rbuf[0]
    for m in range(1, 8):
        total = total + rbuf[m]
    total = total.reshape(96, 128)
    disp[...] = total
    for c in range(3):
        pool[c, 0:32] = total[c * 32:(c + 1) * 32]
        for h in range(16):
            hsend[c, pl.ds(h, 1)] = disp[pl.ds(c * 32 + sent_ref[0, h], 1), :]
    halos = []
    for u in (-1, 0, 1):
        for v in (-1, 0, 1):
            slot = (u + 1) * 3 + v + 1
            if u == 0 and v == 0:
                pool[:, 32 + 16 * slot:48 + 16 * slot] = hsend[...]
                continue
            device = (lax.rem(p - u + 8, 8), lax.rem(q - v + 16, 16))
            halos.append(remote(hsend, pool.at[:, pl.ds(32 + 16 * slot, 16)], hsends.at[slot], hrecv.at[slot], device))
            halos[-1].start()
    for copy in halos:
        copy.wait_recv()
    pool_ref[...] = pool[...]
    for copy in halos:
        copy.wait_send()
    for copy in sends:
        copy.wait_send()
    for m in range(8):
        swap(m).wait_send()

    def drained(step, carry):
        m = lax.rem(group + step, 8)
        remote(sbuf.at[m], rbuf.at[m], rsend.at[m], rrecv.at[m], (p, q)).wait_send()
        return carry

    lax.fori_loop(1, 8, drained, 0)
    for j in range(6):

        @pl.when((8 * j + p) // 6 != p)
        def _():
            remote(sbuf.at[group, j], rbuf.at[group, 0], tsend.at[j], trecv.at[0], (p, q)).wait_send()


def displacement_pool(factor_panel, normals, send_atoms):
    f32, bf16 = jnp.float32, jnp.bfloat16
    dma, regular = pltpu.SemaphoreType.DMA, pltpu.SemaphoreType.REGULAR
    rows, cols = factor_panel.shape
    depth, samples = normals.shape
    return pl.pallas_call(
        displacement_kernel,
        out_shape=jax.ShapeDtypeStruct((3, 176, samples), f32),
        in_specs=[pl.BlockSpec(memory_space=pltpu.HBM), pl.BlockSpec(memory_space=pltpu.HBM), pl.BlockSpec(memory_space=pltpu.HBM)],
        out_specs=pl.BlockSpec(memory_space=pltpu.VMEM),
        scratch_shapes=[
            pltpu.VMEM((8, 2, 8, 96, depth), bf16), pltpu.VMEM((8, depth, samples), bf16),
            pltpu.VMEM((2, 8, 96, samples), f32), pltpu.VMEM((8, 96, samples), f32),
            pltpu.VMEM((8, 6, 16, samples), f32), pltpu.VMEM((8, 6, 16, samples), f32),
            pltpu.VMEM((96, samples), f32), pltpu.VMEM((3, 16, samples), f32), pltpu.VMEM((3, 176, samples), f32),
            dma((8, 2)), dma, dma((14,)), dma((8, 2)), dma((8,)), dma((8,)), dma((8,)), dma((8,)), dma((6,)), dma((6,)), dma((9,)), dma((9,)),
            regular, regular, regular, pltpu.SMEM((1, 16), jnp.int32), dma,
        ],
        compiler_params=pltpu.CompilerParams(collective_id=0, has_side_effects=True, vmem_limit_bytes=48 * 2**20),
        name="displacements",
    )(pltpu.with_memory_space_constraint(send_atoms, pltpu.HBM), factor_panel.reshape(8, 2, 96, cols), pltpu.with_memory_space_constraint(normals, pltpu.HBM))


OMEGA = 90.0 / 127.0
SCALE = math.sqrt(math.log2(math.e)) / OMEGA
MU = 30.0 / 127.0


def pieces(column):
    high = column.astype(jnp.bfloat16)
    rest = column - high.astype(jnp.float32)
    middle = rest.astype(jnp.bfloat16)
    low = (rest - middle.astype(jnp.float32)).astype(jnp.bfloat16)
    return high, middle, low


def beside(weights_t, bias):
    place = lax.broadcasted_iota(jnp.int32, (128, 128), 1)
    high, middle, low = [v.astype(jnp.float32) for v in pieces(bias)]
    extra = jnp.where(place == 0, high, jnp.where(place == 1, middle, jnp.where(place == 2, low, 0.0)))
    return jnp.concatenate([weights_t, extra.astype(jnp.bfloat16)], axis=1)[:, :144]


def pair_kernel(group, nb_ref, bond_ref, pool_ref, w1_ref, b1_ref, w2_ref, b2_ref, ow_ref,
                energy_ref, force_ref, muc_ref, w1a, w2a, w2o):
    atoms = energy_ref.shape[0]
    count = nb_ref.shape[0]
    bf16, f32 = jnp.bfloat16, jnp.float32
    spread = lambda ref: jnp.broadcast_to(ref[...].reshape(1, 128), (128, 128))
    muc_ref[...] = lax.broadcasted_iota(jnp.int32, (128, 128), 0).astype(f32) * (MU * SCALE)
    w1a[...] = beside(w1_ref[...].T, spread(b1_ref).T)
    w2a[...] = beside(w2_ref[...].T, spread(b2_ref).T)
    scaled = (w2_ref[...].astype(f32) * spread(ow_ref)).astype(bf16)
    line = lax.broadcasted_iota(jnp.int32, (16, 128), 0)
    high, middle, low = [v.astype(f32)[:16] for v in pieces(spread(ow_ref))]
    read = jnp.where(line == 0, high, jnp.where(line == 1, middle, jnp.where(line == 2, low, 0.0))).astype(bf16)
    w2o[...] = jnp.concatenate([
        jnp.concatenate([scaled, jnp.zeros((128, 128), bf16)], axis=1),
        jnp.concatenate([jnp.zeros((16, 128), bf16), read], axis=1)], axis=0)
    dot = functools.partial(jnp.dot, preferred_element_type=f32)
    wide = group * count * 128
    ones = jnp.where(lax.broadcasted_iota(jnp.int32, (16, wide), 0) < 3, 1.0, 0.0).astype(bf16)
    at = lambda v, n: v[:, n * 128:(n + 1) * 128]

    def body(k, carry):
        rows, vecs = [], []
        for a in range(group):
            i = k * group + a
            own = [pool_ref[c, pl.ds(i, 1), :] for c in range(3)]
            for n in range(count):
                idx = nb_ref[n, i]
                vec = [pool_ref[c, pl.ds(idx, 1), :] + (bond_ref[c, n, i] - own[c]) for c in range(3)]
                vecs.append(vec)
                rows.append((vec[0] * vec[0] + vec[1] * vec[1] + vec[2] * vec[2]) * SCALE)
        t = jnp.concatenate(rows, axis=1) - jnp.concatenate([muc_ref[...]] * (group * count), axis=1)
        basis = jnp.exp2(-(t * t))
        bt = basis * t
        first = jnp.tanh(dot(w1a[...], jnp.concatenate([basis.astype(bf16), ones], axis=0)))
        second = jnp.tanh(dot(w2a[...], jnp.concatenate([first.astype(bf16), ones], axis=0)))
        slack = (1.0 - second * second).astype(bf16)
        mixed = dot(w2o[...], jnp.concatenate([slack, second.astype(bf16)], axis=0))
        phi = mixed[128:136]
        back1 = (mixed[:128] * (1.0 - first * first)).astype(bf16)
        slope = jnp.sum(dot(w1_ref[...], back1) * bt, axis=0, keepdims=True)
        for a in range(group):
            i = k * group + a
            places = range(a * count, (a + 1) * count)
            energy_ref[pl.ds(i, 1), :] = 0.5 * jnp.sum(sum(at(phi, n) for n in places), axis=0, keepdims=True)
            for c in range(3):
                force_ref[c, pl.ds(i, 1), :] = sum(at(slope, n) * vecs[n][c] for n in places) * (-4.0 / (OMEGA * OMEGA * SCALE))
        return carry

    lax.fori_loop(0, atoms // group, body, 0)


def pair_stage(pool, bond, nb, w1, b1, w2, b2, ow, group=2):
    atoms = bond.shape[1]
    samples = pool.shape[2]
    V = pl.BlockSpec(memory_space=pltpu.VMEM)
    S = pl.BlockSpec(memory_space=pltpu.SMEM)
    f32, bf16 = jnp.float32, jnp.bfloat16
    return pl.pallas_call(
        functools.partial(pair_kernel, group),
        out_shape=(jax.ShapeDtypeStruct((atoms, samples), f32), jax.ShapeDtypeStruct((3, atoms, samples), f32)),
        in_specs=[S, S, V, V, V, V, V, V],
        out_specs=(V, V),
        scratch_shapes=[pltpu.VMEM((128, 128), f32)] + [pltpu.VMEM((128, 144), bf16)] * 2 + [pltpu.VMEM((144, 256), bf16)],
        compiler_params=pltpu.CompilerParams(vmem_limit_bytes=16 * 2**20),
        name="pairs",
    )(nb.T, bond.transpose(0, 2, 1), pool, w1, b1, w2, b2, ow)


def per_device(factor_panel, normals, bond_vectors, neighbours, send_atoms, radial_weight, radial_bias, middle_weight, middle_bias, output_weight):
    pool = displacement_pool(factor_panel, normals, send_atoms)
    return pair_stage(pool, bond_vectors, neighbours, radial_weight, radial_bias, middle_weight, middle_bias, output_weight)


def solution(mesh):
    whole = P(("col", "row"), None)
    return jax.shard_map(
        per_device,
        mesh=mesh,
        in_specs=(P("row", "col"), whole, P(None, ("col", "row"), None), whole, whole, P(), P(), P(), P(), P()),
        out_specs=(whole, P(None, ("col", "row"), None)),
        check_vma=False,
    )
```

```python
import functools
import math

import jax
import jax.numpy as jnp
from jax import lax
from jax.experimental import pallas as pl
from jax.experimental.pallas import tpu as pltpu
from jax.sharding import PartitionSpec as P

MESH = pl.DeviceIdType.MESH


def remote(src, dst, send, recv, device):
    return pltpu.make_async_remote_copy(src_ref=src, dst_ref=dst, send_sem=send, recv_sem=recv, device_id=device, device_id_type=MESH)


def displacement_kernel(sent_hbm, factor_ref, normals_ref, pool_ref, fbuf, nbuf, acc, pbuf, sbuf, rbuf, disp, hsend, pool,
                        fsem, nsem, gsend, grecv, psend, precv, rsend, rrecv, tsend, trecv, hsends, hrecv, y_ready, z_ready, core_ready, sent_ref, sent_sem):
    p, q = lax.axis_index("row"), lax.axis_index("col")
    x, y_lo = lax.rem(p, 4), p // 4
    core, z, y_hi = lax.rem(q, 2), lax.rem(q // 2, 4), q // 8
    at_x = lambda step: y_lo * 4 + lax.rem(x + step, 4)
    other = lambda place: lax.rem(place + 4, 8)
    xp, xm, x2 = at_x(1), at_x(3), at_x(2)
    order = [p, xm, xp, other(p), x2, other(xm), other(xp), other(x2)]
    depth = normals_ref.shape[0]
    third, sixth = depth // 3, depth // 6
    pieces_at = ((0, third), (third, sixth), (third + sixth, sixth), (2 * third, third))

    own = pltpu.make_async_copy(normals_ref, nbuf.at[p], nsem)
    own.start()
    sent_in = pltpu.make_async_copy(sent_hbm, sent_ref, sent_sem)
    sent_in.start()
    loads = []
    for k, place in enumerate(order):
        columns = pl.ds(pl.multiple_of(place * depth, depth), depth)
        loads.append([pltpu.make_async_copy(factor_ref.at[:, side, :, columns], fbuf.at[k, part], fsem.at[k, part])
                      for part, side in enumerate((1 - core, core))])
        for copy in loads[-1]:
            copy.start()

    x_ring = [(at_x(s), q) for s in (1, 2, 3)]
    z_ring = [(p, y_hi * 8 + lax.rem(z + s, 4) * 2 + core) for s in (1, 2, 3)]
    q_flip = lax.rem(q + 8, 16)
    y_ring = [(other(p), q), (p, q_flip), (other(p), q_flip)]
    partner = (p, q + 1 - 2 * core)
    barrier = pltpu.get_barrier_semaphore()
    for device in (*x_ring, *y_ring, *z_ring, partner):
        pl.semaphore_signal(barrier, inc=1, device_id=device, device_id_type=MESH)
    pl.semaphore_wait(barrier, 10)
    for device in y_ring:
        pl.semaphore_signal(y_ready, inc=1, device_id=device, device_id_type=MESH)

    sends = []

    def part(place, h):
        start, size = pieces_at[h]
        return nbuf.at[place, pl.ds(start, size)]

    def push(place, h, device):
        n = len(sends)
        copy = remote(part(place, h), part(place, h), gsend.at[n], grecv.at[place, h], device)
        copy.start()
        sends.append(copy)

    def arrive(place, h):
        remote(part(place, h), part(place, h), gsend.at[0], grecv.at[place, h], (p, q)).wait_recv()

    to_xp, to_xm, to_y = (xp, q), (xm, q), (other(p), q)
    own.wait()
    for a, b, c in ((0, 3, 0), (1, 2, 3), (2, 1, 1), (3, 0, 2)):
        push(p, a, to_xp)
        push(p, b, to_xm)
        push(p, c, to_y)

    def product(cuts, part, first=False):
        left = jnp.concatenate([fbuf[k, part, :, :, start:start + size].reshape(768, size) for k, start, size in cuts], axis=1)
        right = jnp.concatenate([nbuf[order[k], start:start + size] for k, start, size in cuts], axis=0)
        out = jnp.dot(left, right, preferred_element_type=jnp.float32).reshape(8, 96, 128)
        acc[part] = out if first else acc[part] + out

    def multiply(cuts, first=False):
        def half_rows(part, carry):
            product(cuts, part, first)
            return carry

        lax.fori_loop(0, 2, half_rows, 0)

    def chunk(k):
        for copy in loads[k]:
            copy.wait()
        multiply([(k, 0, depth)], k == 0)

    def last(start):
        return [(k, start, third) for k in (5, 6, 7)]

    chunk(0)
    for h in (0, 1):
        arrive(xm, h)
        push(xm, h, to_xp)
        arrive(xp, 3 - h)
        push(xp, 3 - h, to_xm)
    for h in (0, 3, 1, 2):
        arrive(other(p), h)
        push(other(p), h, to_xp)
        push(other(p), h, to_xm)
    for h in (2, 3):
        arrive(xm, h)
        arrive(xp, 3 - h)
    pl.semaphore_wait(y_ready, 3)
    for device in z_ring:
        pl.semaphore_signal(z_ready, inc=1, device_id=device, device_id_type=MESH)
    chunk(1)
    for h in (0, 3):
        arrive(x2, h)
        push(x2, h, to_y)
    chunk(2)
    for h in (1, 2):
        arrive(x2, h)
        push(x2, h, to_y)
    chunk(3)
    chunk(4)
    pl.semaphore_wait(z_ready, 3)
    pl.semaphore_signal(core_ready, inc=1, device_id=partner, device_id_type=MESH)
    for k in (5, 6, 7):
        for copy in loads[k]:
            copy.wait()
    for h, start in ((0, 0), (3, 2 * third)):
        for place in (other(xm), other(xp), other(x2)):
            arrive(place, h)
        multiply(last(start))
    for h in (1, 2):
        for place in (other(xm), other(xp), other(x2)):
            arrive(place, h)
    group = q // 2

    def ahead(step):
        late = step // 4
        shift = (1 - late) * lax.rem(2 + step, 4) + late * (1 + lax.rem(step, 3))
        return lax.rem(y_hi + 1 - late, 2) * 4 + lax.rem(z + shift, 4)

    def swap(m):
        return remote(acc.at[0, m], pbuf.at[m], psend.at[m], precv.at[m], partner)

    product(last(third), 0)

    def swap_out(step, carry):
        swap(ahead(step)).start()
        return carry

    lax.fori_loop(0, 7, swap_out, 0)
    swap(group).start()
    product(last(third), 1)
    pl.semaphore_wait(core_ready, 1)

    def spread(step, carry):
        m = ahead(step)
        swap(m).wait_recv()
        sbuf[m] = (acc[1, m] + pbuf[m]).reshape(6, 16, 128)
        for j in range(6):
            tile = 8 * j + p
            owner, place = tile // 6, lax.rem(tile, 6)
            remote(sbuf.at[m, j], rbuf.at[group, place], rsend.at[m], rrecv.at[group], (owner, 2 * m + core)).start()
        return carry

    lax.fori_loop(0, 7, spread, 0)
    swap(group).wait_recv()
    sbuf[group] = (acc[1, group] + pbuf[group]).reshape(6, 16, 128)
    for j in range(6):
        tile = 8 * j + p
        owner, place = tile // 6, lax.rem(tile, 6)

        @pl.when(owner == p)
        def _():
            pltpu.make_async_copy(sbuf.at[group, j], rbuf.at[group, place], trecv.at[place]).start()

        @pl.when(owner != p)
        def _():
            remote(sbuf.at[group, j], rbuf.at[group, place], tsend.at[j], trecv.at[place], (owner, q)).start()

    for i in range(6):
        pltpu.make_async_copy(sbuf.at[group, 0], rbuf.at[group, i], trecv.at[i]).wait()

    def landed(step, carry):
        m = lax.rem(group + step, 8)
        remote(sbuf.at[m], rbuf.at[m], rsend.at[m], rrecv.at[m], (p, q)).wait_recv()
        return carry

    lax.fori_loop(1, 8, landed, 0)
    sent_in.wait()
    total = rbuf[0]
    for m in range(1, 8):
        total = total + rbuf[m]
    total = total.reshape(96, 128)
    disp[...] = total
    for c in range(3):
        pool[c, 0:32] = total[c * 32:(c + 1) * 32]
        for h in range(16):
            hsend[c, pl.ds(h, 1)] = disp[pl.ds(c * 32 + sent_ref[0, h], 1), :]
    halos = []
    pool[:, 32 + 64:48 + 64] = hsend[...]
    for u, v in ((-1, -1), (1, 1), (-1, 1), (1, -1), (-1, 0), (1, 0), (0, -1), (0, 1)):
        slot = (u + 1) * 3 + v + 1
        device = (lax.rem(p - u + 8, 8), lax.rem(q - v + 16, 16))
        halos.append(remote(hsend, pool.at[:, pl.ds(32 + 16 * slot, 16)], hsends.at[slot], hrecv.at[slot], device))
        halos[-1].start()
    for copy in halos:
        copy.wait_recv()
    pool_ref[...] = pool[...]
    for copy in halos:
        copy.wait_send()
    for copy in sends:
        copy.wait_send()
    for m in range(8):
        swap(m).wait_send()

    def drained(step, carry):
        m = lax.rem(group + step, 8)
        remote(sbuf.at[m], rbuf.at[m], rsend.at[m], rrecv.at[m], (p, q)).wait_send()
        return carry

    lax.fori_loop(1, 8, drained, 0)
    for j in range(6):

        @pl.when((8 * j + p) // 6 != p)
        def _():
            remote(sbuf.at[group, j], rbuf.at[group, 0], tsend.at[j], trecv.at[0], (p, q)).wait_send()


def displacement_pool(factor_panel, normals, send_atoms):
    f32, bf16 = jnp.float32, jnp.bfloat16
    dma, regular = pltpu.SemaphoreType.DMA, pltpu.SemaphoreType.REGULAR
    rows, cols = factor_panel.shape
    depth, samples = normals.shape
    return pl.pallas_call(
        displacement_kernel,
        out_shape=jax.ShapeDtypeStruct((3, 176, samples), f32),
        in_specs=[pl.BlockSpec(memory_space=pltpu.HBM), pl.BlockSpec(memory_space=pltpu.HBM), pl.BlockSpec(memory_space=pltpu.HBM)],
        out_specs=pl.BlockSpec(memory_space=pltpu.VMEM),
        scratch_shapes=[
            pltpu.VMEM((8, 2, 8, 96, depth), bf16), pltpu.VMEM((8, depth, samples), bf16),
            pltpu.VMEM((2, 8, 96, samples), f32), pltpu.VMEM((8, 96, samples), f32),
            pltpu.VMEM((8, 6, 16, samples), f32), pltpu.VMEM((8, 6, 16, samples), f32),
            pltpu.VMEM((96, samples), f32), pltpu.VMEM((3, 16, samples), f32), pltpu.VMEM((3, 176, samples), f32),
            dma((8, 2)), dma, dma((28,)), dma((8, 4)), dma((8,)), dma((8,)), dma((8,)), dma((8,)), dma((6,)), dma((6,)), dma((9,)), dma((9,)),
            regular, regular, regular, pltpu.SMEM((1, 16), jnp.int32), dma,
        ],
        compiler_params=pltpu.CompilerParams(collective_id=0, has_side_effects=True, vmem_limit_bytes=48 * 2**20),
        name="displacements",
    )(pltpu.with_memory_space_constraint(send_atoms, pltpu.HBM), factor_panel.reshape(8, 2, 96, cols), pltpu.with_memory_space_constraint(normals, pltpu.HBM))


OMEGA = 90.0 / 127.0
SCALE = math.sqrt(math.log2(math.e)) / OMEGA
MU = 30.0 / 127.0


def pieces(column):
    high = column.astype(jnp.bfloat16)
    rest = column - high.astype(jnp.float32)
    middle = rest.astype(jnp.bfloat16)
    low = (rest - middle.astype(jnp.float32)).astype(jnp.bfloat16)
    return high, middle, low


def beside(weights_t, bias):
    place = lax.broadcasted_iota(jnp.int32, (128, 128), 1)
    high, middle, low = [v.astype(jnp.float32) for v in pieces(bias)]
    extra = jnp.where(place == 0, high, jnp.where(place == 1, middle, jnp.where(place == 2, low, 0.0)))
    return jnp.concatenate([weights_t, extra.astype(jnp.bfloat16)], axis=1)[:, :144]


def pair_kernel(pairs, nb_ref, bond_ref, pool_ref, w1_ref, b1_ref, w2_ref, b2_ref, ow_ref,
                energy_ref, force_ref, ow_s, muc_ref, w1a, w2a, vec_s, sq_s, phi_s):
    atoms = energy_ref.shape[0]
    count = nb_ref.shape[0]
    bf16, f32 = jnp.bfloat16, jnp.float32
    spread = lambda ref: jnp.broadcast_to(ref[...].reshape(1, 128), (128, 128))
    muc_ref[...] = lax.broadcasted_iota(jnp.int32, (128, 128), 0).astype(f32) * (MU * SCALE)
    w1a[...] = beside(w1_ref[...].T, spread(b1_ref).T)
    w2a[...] = beside(w2_ref[...].T, spread(b2_ref).T)
    ow_s[...] = spread(ow_ref).T
    dot = functools.partial(jnp.dot, preferred_element_type=f32)
    at = lambda v, n: v[:, n * 128:(n + 1) * 128]

    def gather(n, carry):
        base = pl.multiple_of(n * atoms, atoms)
        for i in range(atoms):
            idx = nb_ref[n, i]
            for c in range(3):
                vec_s[c, pl.ds(base + i, 1), :] = pool_ref[c, pl.ds(idx, 1), :] + bond_ref[c, n, i]
        square = jnp.zeros((atoms, 128), f32)
        for c in range(3):
            vec = vec_s[c, pl.ds(base, atoms), :] - pool_ref[c, 0:atoms, :]
            vec_s[c, pl.ds(base, atoms), :] = vec
            square = square + vec * vec
        sq_s[pl.ds(base, atoms), :] = square * SCALE
        return carry

    lax.fori_loop(0, count, gather, 0)
    ones = jnp.where(lax.broadcasted_iota(jnp.int32, (16, pairs * 128), 0) < 3, 1.0, 0.0).astype(bf16)

    def body(k, carry):
        base = pl.multiple_of(k * pairs, pairs)
        sq = jnp.concatenate([sq_s[pl.ds(base + n, 1), :] for n in range(pairs)], axis=1)
        t = sq - jnp.concatenate([muc_ref[...]] * pairs, axis=1)
        ow = jnp.concatenate([ow_s[...]] * (pairs), axis=1)
        basis = jnp.exp2(-(t * t))
        bt = basis * t
        first = jnp.tanh(dot(w1a[...], jnp.concatenate([basis.astype(bf16), ones], axis=0)))
        second = jnp.tanh(dot(w2a[...], jnp.concatenate([first.astype(bf16), ones], axis=0)))
        so = second * ow
        slack = (ow - second * so).astype(bf16)
        phi = jnp.sum(so, axis=0, keepdims=True)
        back1 = (dot(w2_ref[...], slack) * (1.0 - first * first)).astype(bf16)
        slope = jnp.sum(dot(w1_ref[...], back1) * bt, axis=0, keepdims=True)
        for n in range(pairs):
            phi_s[pl.ds(base + n, 1), :] = at(phi, n)
            sq_s[pl.ds(base + n, 1), :] = at(slope, n)
        return carry

    lax.fori_loop(0, count * atoms // pairs, body, 0)
    energy = jnp.zeros((atoms, 128), f32)
    force = [jnp.zeros((atoms, 128), f32) for _ in range(3)]
    for n in range(count):
        rows = pl.ds(n * atoms, atoms)
        energy = energy + phi_s[rows, :]
        for c in range(3):
            force[c] = force[c] + sq_s[rows, :] * vec_s[c, rows, :]
    energy_ref[...] = 0.5 * energy
    for c in range(3):
        force_ref[c] = force[c] * (-4.0 / (OMEGA * OMEGA * SCALE))


def pair_stage(pool, bond, nb, w1, b1, w2, b2, ow, pairs=24):
    atoms = bond.shape[1]
    samples = pool.shape[2]
    V = pl.BlockSpec(memory_space=pltpu.VMEM)
    S = pl.BlockSpec(memory_space=pltpu.SMEM)
    f32, bf16 = jnp.float32, jnp.bfloat16
    return pl.pallas_call(
        functools.partial(pair_kernel, pairs),
        out_shape=(jax.ShapeDtypeStruct((atoms, samples), f32), jax.ShapeDtypeStruct((3, atoms, samples), f32)),
        in_specs=[S, S, V, V, V, V, V, V],
        out_specs=(V, V),
        scratch_shapes=[pltpu.VMEM((128, 128), f32)] * 2 + [pltpu.VMEM((128, 144), bf16)] * 2 + [pltpu.VMEM((3, 384, samples), f32), pltpu.VMEM((384, samples), f32), pltpu.VMEM((384, samples), f32)],
        compiler_params=pltpu.CompilerParams(vmem_limit_bytes=16 * 2**20),
        name="pairs",
    )(nb.T, bond.transpose(0, 2, 1), pool, w1, b1, w2, b2, ow)


def per_device(factor_panel, normals, bond_vectors, neighbours, send_atoms, radial_weight, radial_bias, middle_weight, middle_bias, output_weight):
    pool = displacement_pool(factor_panel, normals, send_atoms)
    return pair_stage(pool, bond_vectors, neighbours, radial_weight, radial_bias, middle_weight, middle_bias, output_weight)


def solution(mesh):
    whole = P(("col", "row"), None)
    return jax.shard_map(
        per_device,
        mesh=mesh,
        in_specs=(P("row", "col"), whole, P(None, ("col", "row"), None), whole, whole, P(), P(), P(), P(), P()),
        out_specs=(whole, P(None, ("col", "row"), None)),
        check_vma=False,
    )
```

```python
import functools
import math

import jax
import jax.numpy as jnp
from jax import lax
from jax.experimental import pallas as pl
from jax.experimental.pallas import tpu as pltpu
from jax.sharding import PartitionSpec as P

MESH = pl.DeviceIdType.MESH


def remote(src, dst, send, recv, device):
    return pltpu.make_async_remote_copy(src_ref=src, dst_ref=dst, send_sem=send, recv_sem=recv, device_id=device, device_id_type=MESH)


def displacement_kernel(sent_hbm, factor_ref, normals_ref, pool_ref, fbuf, nbuf, acc, pbuf, sbuf, rbuf, disp, hsend, pool,
                        fsem, nsem, gsend, grecv, psend, precv, rsend, rrecv, tsend, trecv, hsends, hrecv, y_ready, z_ready, core_ready, sent_ref, sent_sem):
    p, q = lax.axis_index("row"), lax.axis_index("col")
    x, y_lo = lax.rem(p, 4), p // 4
    core, z, y_hi = lax.rem(q, 2), lax.rem(q // 2, 4), q // 8
    at_x = lambda step: y_lo * 4 + lax.rem(x + step, 4)
    other = lambda place: lax.rem(place + 4, 8)
    xp, xm, x2 = at_x(1), at_x(3), at_x(2)
    order = [p, xm, xp, other(p), x2, other(xm), other(xp), other(x2)]
    depth = normals_ref.shape[0]
    third, sixth = depth // 3, depth // 6
    pieces_at = ((0, third), (third, sixth), (third + sixth, sixth), (2 * third, third))

    own = pltpu.make_async_copy(normals_ref, nbuf.at[p], nsem)
    own.start()
    sent_in = pltpu.make_async_copy(sent_hbm, sent_ref, sent_sem)
    sent_in.start()
    loads = []
    for k, place in enumerate(order):
        columns = pl.ds(pl.multiple_of(place * depth, depth), depth)
        loads.append([pltpu.make_async_copy(factor_ref.at[:, side, :, columns], fbuf.at[k, part], fsem.at[k, part])
                      for part, side in enumerate((1 - core, core))])
        for copy in loads[-1]:
            copy.start()

    x_ring = [(at_x(s), q) for s in (1, 2, 3)]
    z_ring = [(p, y_hi * 8 + lax.rem(z + s, 4) * 2 + core) for s in (1, 2, 3)]
    q_flip = lax.rem(q + 8, 16)
    y_ring = [(other(p), q), (p, q_flip), (other(p), q_flip)]
    partner = (p, q + 1 - 2 * core)
    barrier = pltpu.get_barrier_semaphore()
    for device in (*x_ring, *y_ring, *z_ring, partner):
        pl.semaphore_signal(barrier, inc=1, device_id=device, device_id_type=MESH)
    pl.semaphore_wait(barrier, 10)
    for device in y_ring:
        pl.semaphore_signal(y_ready, inc=1, device_id=device, device_id_type=MESH)

    sends = []

    def part(place, h):
        start, size = pieces_at[h]
        return nbuf.at[place, pl.ds(start, size)]

    def push(place, h, device):
        n = len(sends)
        copy = remote(part(place, h), part(place, h), gsend.at[n], grecv.at[place, h], device)
        copy.start()
        sends.append(copy)

    def arrive(place, h):
        remote(part(place, h), part(place, h), gsend.at[0], grecv.at[place, h], (p, q)).wait_recv()

    to_xp, to_xm, to_y = (xp, q), (xm, q), (other(p), q)
    own.wait()
    for a, b, c in ((0, 3, 0), (1, 2, 3), (2, 1, 1), (3, 0, 2)):
        push(p, a, to_xp)
        push(p, b, to_xm)
        push(p, c, to_y)

    def product(cuts, part, first=False):
        left = jnp.concatenate([fbuf[k, part, :, :, start:start + size].reshape(768, size) for k, start, size in cuts], axis=1)
        right = jnp.concatenate([nbuf[order[k], start:start + size] for k, start, size in cuts], axis=0)
        out = jnp.dot(left, right, preferred_element_type=jnp.float32).reshape(8, 96, 128)
        acc[part] = out if first else acc[part] + out

    def multiply(cuts, first=False):
        def half_rows(part, carry):
            product(cuts, part, first)
            return carry

        lax.fori_loop(0, 2, half_rows, 0)

    def chunk(k):
        for copy in loads[k]:
            copy.wait()
        multiply([(k, 0, depth)], k == 0)

    def last(start):
        return [(k, start, third) for k in (5, 6, 7)]

    chunk(0)
    for h in (0, 1):
        arrive(xm, h)
        push(xm, h, to_xp)
        arrive(xp, 3 - h)
        push(xp, 3 - h, to_xm)
    for h in (0, 3, 1, 2):
        arrive(other(p), h)
        push(other(p), h, to_xp)
        push(other(p), h, to_xm)
    for h in (2, 3):
        arrive(xm, h)
        arrive(xp, 3 - h)
    pl.semaphore_wait(y_ready, 3)
    for device in z_ring:
        pl.semaphore_signal(z_ready, inc=1, device_id=device, device_id_type=MESH)
    chunk(1)
    for h in (0, 3):
        arrive(x2, h)
        push(x2, h, to_y)
    chunk(2)
    for h in (1, 2):
        arrive(x2, h)
        push(x2, h, to_y)
    chunk(3)
    chunk(4)
    pl.semaphore_wait(z_ready, 3)
    pl.semaphore_signal(core_ready, inc=1, device_id=partner, device_id_type=MESH)
    for k in (5, 6, 7):
        for copy in loads[k]:
            copy.wait()
    for h, start in ((0, 0), (3, 2 * third)):
        for place in (other(xm), other(xp), other(x2)):
            arrive(place, h)
        multiply(last(start))
    for h in (1, 2):
        for place in (other(xm), other(xp), other(x2)):
            arrive(place, h)
    group = q // 2

    def ahead(step):
        late = step // 4
        shift = (1 - late) * lax.rem(2 + step, 4) + late * (1 + lax.rem(step, 3))
        return lax.rem(y_hi + 1 - late, 2) * 4 + lax.rem(z + shift, 4)

    def swap(m):
        return remote(acc.at[0, m], pbuf.at[m], psend.at[m], precv.at[m], partner)

    product(last(third), 0)

    def swap_out(step, carry):
        swap(ahead(step)).start()
        return carry

    lax.fori_loop(0, 7, swap_out, 0)
    swap(group).start()
    product(last(third), 1)
    pl.semaphore_wait(core_ready, 1)

    def spread(step, carry):
        m = ahead(step)
        swap(m).wait_recv()
        sbuf[m] = (acc[1, m] + pbuf[m]).reshape(6, 16, 128)
        for j in range(6):
            tile = 8 * j + p
            owner, place = tile // 6, lax.rem(tile, 6)
            remote(sbuf.at[m, j], rbuf.at[group, place], rsend.at[m], rrecv.at[group], (owner, 2 * m + core)).start()
        return carry

    lax.fori_loop(0, 7, spread, 0)
    swap(group).wait_recv()
    sbuf[group] = (acc[1, group] + pbuf[group]).reshape(6, 16, 128)
    for j in range(6):
        tile = 8 * j + p
        owner, place = tile // 6, lax.rem(tile, 6)

        @pl.when(owner == p)
        def _():
            pltpu.make_async_copy(sbuf.at[group, j], rbuf.at[group, place], trecv.at[place]).start()

        @pl.when(owner != p)
        def _():
            remote(sbuf.at[group, j], rbuf.at[group, place], tsend.at[j], trecv.at[place], (owner, q)).start()

    for i in range(6):
        pltpu.make_async_copy(sbuf.at[group, 0], rbuf.at[group, i], trecv.at[i]).wait()

    def landed(step, carry):
        m = lax.rem(group + step, 8)
        remote(sbuf.at[m], rbuf.at[m], rsend.at[m], rrecv.at[m], (p, q)).wait_recv()
        return carry

    lax.fori_loop(1, 8, landed, 0)
    sent_in.wait()
    total = rbuf[0]
    for m in range(1, 8):
        total = total + rbuf[m]
    total = total.reshape(96, 128)
    disp[...] = total
    for c in range(3):
        pool[c, 0:32] = total[c * 32:(c + 1) * 32]
        for h in range(16):
            hsend[c, pl.ds(h, 1)] = disp[pl.ds(c * 32 + sent_ref[0, h], 1), :]
    halos = []
    pool[:, 32 + 64:48 + 64] = hsend[...]
    for u, v in ((-1, -1), (1, 1), (-1, 1), (1, -1), (-1, 0), (1, 0), (0, -1), (0, 1)):
        slot = (u + 1) * 3 + v + 1
        device = (lax.rem(p - u + 8, 8), lax.rem(q - v + 16, 16))
        halos.append(remote(hsend, pool.at[:, pl.ds(32 + 16 * slot, 16)], hsends.at[slot], hrecv.at[slot], device))
        halos[-1].start()
    for copy in halos:
        copy.wait_recv()
    pool_ref[...] = pool[...]
    for copy in halos:
        copy.wait_send()
    for copy in sends:
        copy.wait_send()
    for m in range(8):
        swap(m).wait_send()

    def drained(step, carry):
        m = lax.rem(group + step, 8)
        remote(sbuf.at[m], rbuf.at[m], rsend.at[m], rrecv.at[m], (p, q)).wait_send()
        return carry

    lax.fori_loop(1, 8, drained, 0)
    for j in range(6):

        @pl.when((8 * j + p) // 6 != p)
        def _():
            remote(sbuf.at[group, j], rbuf.at[group, 0], tsend.at[j], trecv.at[0], (p, q)).wait_send()


def displacement_pool(factor_panel, normals, send_atoms):
    f32, bf16 = jnp.float32, jnp.bfloat16
    dma, regular = pltpu.SemaphoreType.DMA, pltpu.SemaphoreType.REGULAR
    rows, cols = factor_panel.shape
    depth, samples = normals.shape
    return pl.pallas_call(
        displacement_kernel,
        out_shape=jax.ShapeDtypeStruct((3, 176, samples), f32),
        in_specs=[pl.BlockSpec(memory_space=pltpu.HBM), pl.BlockSpec(memory_space=pltpu.HBM), pl.BlockSpec(memory_space=pltpu.HBM)],
        out_specs=pl.BlockSpec(memory_space=pltpu.VMEM),
        scratch_shapes=[
            pltpu.VMEM((8, 2, 8, 96, depth), bf16), pltpu.VMEM((8, depth, samples), bf16),
            pltpu.VMEM((2, 8, 96, samples), f32), pltpu.VMEM((8, 96, samples), f32),
            pltpu.VMEM((8, 6, 16, samples), f32), pltpu.VMEM((8, 6, 16, samples), f32),
            pltpu.VMEM((96, samples), f32), pltpu.VMEM((3, 16, samples), f32), pltpu.VMEM((3, 176, samples), f32),
            dma((8, 2)), dma, dma((28,)), dma((8, 4)), dma((8,)), dma((8,)), dma((8,)), dma((8,)), dma((6,)), dma((6,)), dma((9,)), dma((9,)),
            regular, regular, regular, pltpu.SMEM((1, 16), jnp.int32), dma,
        ],
        compiler_params=pltpu.CompilerParams(collective_id=0, has_side_effects=True, vmem_limit_bytes=48 * 2**20),
        name="displacements",
    )(pltpu.with_memory_space_constraint(send_atoms, pltpu.HBM), factor_panel.reshape(8, 2, 96, cols), pltpu.with_memory_space_constraint(normals, pltpu.HBM))


OMEGA = 90.0 / 127.0
SCALE = math.sqrt(math.log2(math.e)) / OMEGA
MU = 30.0 / 127.0


def pieces(column):
    high = column.astype(jnp.bfloat16)
    rest = column - high.astype(jnp.float32)
    middle = rest.astype(jnp.bfloat16)
    low = (rest - middle.astype(jnp.float32)).astype(jnp.bfloat16)
    return high, middle, low


def beside(weights_t, bias):
    place = lax.broadcasted_iota(jnp.int32, (128, 128), 1)
    high, middle, low = [v.astype(jnp.float32) for v in pieces(bias)]
    extra = jnp.where(place == 0, high, jnp.where(place == 1, middle, jnp.where(place == 2, low, 0.0)))
    return jnp.concatenate([weights_t, extra.astype(jnp.bfloat16)], axis=1)[:, :144]


def pair_kernel(pairs, nb_ref, bond_ref, pool_ref, w1_ref, b1_ref, w2_ref, b2_ref, ow_ref,
                energy_ref, force_ref, ow_s, muc_ref, w1a, w2a, vec_s, sq_s, phi_s):
    atoms = energy_ref.shape[0]
    count = nb_ref.shape[0]
    bf16, f32 = jnp.bfloat16, jnp.float32
    spread = lambda ref: jnp.broadcast_to(ref[...].reshape(1, 128), (128, 128))
    muc_ref[...] = lax.broadcasted_iota(jnp.int32, (128, 128), 0).astype(f32) * (MU * SCALE)
    w1a[...] = beside(w1_ref[...].T, spread(b1_ref).T)
    w2a[...] = beside(w2_ref[...].T, spread(b2_ref).T)
    ow_s[...] = spread(ow_ref).T
    dot = functools.partial(jnp.dot, preferred_element_type=f32)
    at = lambda v, n: v[:, n * 128:(n + 1) * 128]

    bonds = [bond_ref[c].T for c in range(3)]
    for n in range(count):
        base = n * atoms
        for i in range(atoms):
            idx = nb_ref[n, i]
            for c in range(3):
                vec_s[c, base + i:base + i + 1, :] = pool_ref[c, pl.ds(idx, 1), :]
        square = jnp.zeros((atoms, 128), f32)
        for c in range(3):
            vec = bonds[c][:, n:n + 1] + vec_s[c, base:base + atoms, :] - pool_ref[c, 0:atoms, :]
            vec_s[c, base:base + atoms, :] = vec
            square = square + vec * vec
        sq_s[base:base + atoms, :] = square * SCALE

    ones = jnp.where(lax.broadcasted_iota(jnp.int32, (16, pairs * 128), 0) < 3, 1.0, 0.0).astype(bf16)

    def body(k, carry):
        base = pl.multiple_of(k * pairs, pairs)
        sq = jnp.concatenate([sq_s[pl.ds(base + n, 1), :] for n in range(pairs)], axis=1)
        t = sq - jnp.concatenate([muc_ref[...]] * pairs, axis=1)
        ow = jnp.concatenate([ow_s[...]] * (pairs), axis=1)
        basis = jnp.exp2(-(t * t))
        bt = basis * t
        first = jnp.tanh(dot(w1a[...], jnp.concatenate([basis.astype(bf16), ones], axis=0)))
        second = jnp.tanh(dot(w2a[...], jnp.concatenate([first.astype(bf16), ones], axis=0)))
        so = second * ow
        slack = (ow - second * so).astype(bf16)
        phi = jnp.sum(so, axis=0, keepdims=True)
        back1 = (dot(w2_ref[...], slack) * (1.0 - first * first)).astype(bf16)
        slope = jnp.sum(dot(w1_ref[...], back1) * bt, axis=0, keepdims=True)
        for n in range(pairs):
            phi_s[pl.ds(base + n, 1), :] = at(phi, n)
            sq_s[pl.ds(base + n, 1), :] = at(slope, n)
        return carry

    lax.fori_loop(0, count * atoms // pairs, body, 0)
    energy = jnp.zeros((atoms, 128), f32)
    force = [jnp.zeros((atoms, 128), f32) for _ in range(3)]
    for n in range(count):
        rows = pl.ds(n * atoms, atoms)
        energy = energy + phi_s[rows, :]
        for c in range(3):
            force[c] = force[c] + sq_s[rows, :] * vec_s[c, rows, :]
    energy_ref[...] = 0.5 * energy
    for c in range(3):
        force_ref[c] = force[c] * (-4.0 / (OMEGA * OMEGA * SCALE))


def pair_stage(pool, bond, nb, w1, b1, w2, b2, ow, pairs=24):
    atoms = bond.shape[1]
    samples = pool.shape[2]
    V = pl.BlockSpec(memory_space=pltpu.VMEM)
    S = pl.BlockSpec(memory_space=pltpu.SMEM)
    f32, bf16 = jnp.float32, jnp.bfloat16
    return pl.pallas_call(
        functools.partial(pair_kernel, pairs),
        out_shape=(jax.ShapeDtypeStruct((atoms, samples), f32), jax.ShapeDtypeStruct((3, atoms, samples), f32)),
        in_specs=[S, V, V, V, V, V, V, V],
        out_specs=(V, V),
        scratch_shapes=[pltpu.VMEM((128, 128), f32)] * 2 + [pltpu.VMEM((128, 144), bf16)] * 2 + [pltpu.VMEM((3, 384, samples), f32), pltpu.VMEM((384, samples), f32), pltpu.VMEM((384, samples), f32)],
        compiler_params=pltpu.CompilerParams(vmem_limit_bytes=16 * 2**20),
        name="pairs",
    )(nb.T, bond.transpose(0, 2, 1), pool, w1, b1, w2, b2, ow)


def per_device(factor_panel, normals, bond_vectors, neighbours, send_atoms, radial_weight, radial_bias, middle_weight, middle_bias, output_weight):
    pool = displacement_pool(factor_panel, normals, send_atoms)
    return pair_stage(pool, bond_vectors, neighbours, radial_weight, radial_bias, middle_weight, middle_bias, output_weight)


def solution(mesh):
    whole = P(("col", "row"), None)
    return jax.shard_map(
        per_device,
        mesh=mesh,
        in_specs=(P("row", "col"), whole, P(None, ("col", "row"), None), whole, whole, P(), P(), P(), P(), P()),
        out_specs=(whole, P(None, ("col", "row"), None)),
        check_vma=False,
    )
```
